1024 devices in a mesh: blk: 32 (over z_lo, core), uly: 32 (over y, x, z_hi).
Axes of the slice: x: 4, y: 4, z: 32 (z_hi: 2, z_lo: 16; z = z_hi * 16 + z_lo), core: 2. Of those that a mesh axis runs over, the one named last changes fastest.
Arguments:
- queries: bfloat16 [32768, 32, 128], P(('blk', 'uly')), may hold values from -6 to 6
- keys: bfloat16 [32768, 4, 128], P(('blk', 'uly')), may hold values from -6 to 6
- values: bfloat16 [32768, 4, 128], P(('blk', 'uly')), may hold values from -6 to 6
- grad_out: bfloat16 [32768, 32, 128], P(('blk', 'uly')), may hold values from -6 to 6
- stats: bfloat16 [32768, 32, 2], P(('blk', 'uly')), as said below
- placement: int32 [64], replicated, may hold values from 0 to 63, as said below
Outputs:
- grad_queries: bfloat16 [32768, 32, 128], P(('blk', 'uly'))
- key_accum: float32 [32768, 32, 128], P('blk', 'uly')
- value_accum: float32 [32768, 32, 128], P('blk', 'uly')
The draws below stay inside these ranges and needn't reach their ends.
Inputs may be any that keep to these rules, and one draw needn't show every extreme that they name: `placement`: entries 2 b and 2 b + 1 are, in some order, r and 63 - r for some r < 32; each number of 0 to 63 appears once. `stats`: the first entry is the log of a softmax total of the forward pass; the second the row sum of the output gradient times the output.
All inputs are finite; a program needn't handle non-finite values.
Results may differ from the reference program's by a relative error of at most 0.007.
Values may be sent and summed in bfloat16 or wider, within the bound.
A program may use at most 32 MiB of HBM per device.

```python
import jax
import jax.numpy as jnp
from jax import lax

H = 32
KVH = 4
DH = 128
SBLK = 1024
TOKENS = 32768
SPANS = 64
N_BLK = 32


def shared_placement(key):
    key_one, key_two = jax.random.split(jax.random.fold_in(key, 11))
    half_count = SPANS // 2
    ranks = jax.random.permutation(key_one, half_count).astype(jnp.int32)
    flipped = jax.random.randint(key_two, (half_count,), 0, 2).astype(jnp.int32)
    lower = ranks
    upper = (SPANS - 1 - ranks).astype(jnp.int32)
    first = jnp.where(flipped == 1, upper, lower)
    second = jnp.where(flipped == 1, lower, upper)
    return jnp.stack([first, second], axis=1).reshape(SPANS).astype(jnp.int32)


def draw_stats(key, part):
    key_one, key_two = jax.random.split(jax.random.fold_in(key, 7))
    extent = (TOKENS, H)
    piece_len = SBLK // 2
    block_count = SPANS // 2
    pairs = shared_placement(key).reshape(block_count, 2)
    window = jnp.concatenate([pairs, jnp.roll(pairs, 1, axis=0)], axis=1) * piece_len
    positions = (pairs[:, :, None] * piece_len + jnp.arange(piece_len, dtype=jnp.int32)[None, None, :]).reshape(block_count, SBLK)
    seen = jnp.sum(jnp.clip(positions[:, :, None] - window[:, None, :] + 1, 0, piece_len), axis=2)
    log_count = jnp.log(seen.astype(jnp.float32)).reshape(TOKENS, 1)
    offset = jax.random.uniform(key_one, extent, jnp.float32, -0.5, 0.5)
    correction = jnp.clip(3.0 * jax.random.normal(key_two, extent, jnp.float32), -9.0, 9.0)
    log_norm = 0.5 * log_count + 1.0 + offset
    return jnp.stack([log_norm, correction], axis=-1).astype(jnp.bfloat16)


def draw_placement(key, part):
    return shared_placement(key)


def levels(key, shape, cuts, low, top_value):
    def one(position, shards_of):
        draws = jax.random.uniform(jax.random.fold_in(jax.random.fold_in(key, 6), position), (shards_of,), jnp.float32, low / len(cuts), top_value / len(cuts))
        return jnp.repeat(jnp.exp(draws), shape[position] // shards_of).reshape((-1,) + (1,) * (len(shape) - position - 1))

    loudness = one(*cuts[0])
    for cut in cuts[1:]:
        loudness = loudness * one(*cut)
    return loudness


def gaussian(stream_key, dims, scale, bound, pieces=(), kind=jnp.bfloat16):
    result = jax.random.normal(stream_key, dims, jnp.float32) * scale
    if len(pieces) > 0:
        result = levels(stream_key, dims, pieces, -0.22, 0.18) * result
    return jnp.clip(result, min=-bound, max=bound).astype(kind)


def setup_inputs(seed: int = 0) -> dict:
    seeds = jax.random.split(jax.random.key(seed), 7)
    return {
        "queries": gaussian(seeds[0], (TOKENS, H, DH), 1.0, 6.0, ((0, 1024),)),
        "keys": gaussian(seeds[1], (TOKENS, KVH, DH), 1.0, 6.0, ((0, 1024),)),
        "values": gaussian(seeds[2], (TOKENS, KVH, DH), 1.0, 6.0, ((0, 1024),)),
        "grad_out": gaussian(seeds[3], (TOKENS, H, DH), 1.0, 6.0, ((0, 1024),)),
        "stats": draw_stats(jax.random.fold_in(seeds[6], 71), 0),
        "placement": draw_placement(jax.random.fold_in(seeds[6], 71), 0),
    }


def block_grads(query_blk, grad_blk, stat_blk, key_blk, value_blk, query_pos, key_pos):
    factor = DH ** -0.5
    scores = jnp.einsum("qhd,khd->hqk", query_blk.astype(jnp.float32), key_blk.astype(jnp.float32)) * factor
    log_norm = stat_blk[:, :, 0].astype(jnp.float32).T[:, :, None]
    correction = stat_blk[:, :, 1].astype(jnp.float32).T[:, :, None]
    allowed = key_pos[None, :] <= query_pos[:, None]
    weights = jnp.where(allowed[None], jnp.exp(scores - log_norm), 0.0)
    weights_low = weights.astype(jnp.bfloat16).astype(jnp.float32)
    grad_value = jnp.einsum("hqk,qhd->khd", weights_low, grad_blk.astype(jnp.float32))
    grad_weights = jnp.einsum("qhd,khd->hqk", grad_blk.astype(jnp.float32), value_blk.astype(jnp.float32))
    grad_scores = (weights * (grad_weights - correction)).astype(jnp.bfloat16).astype(jnp.float32)
    grad_query = jnp.einsum("hqk,khd->qhd", grad_scores, key_blk.astype(jnp.float32)) * factor
    grad_key = jnp.einsum("hqk,qhd->khd", grad_scores, query_blk.astype(jnp.float32)) * factor
    return grad_query, grad_key, grad_value


def reference(queries, keys, values, grad_out, stats, placement):
    piece_len = SBLK // 2
    repeats = H // KVH
    query_all = queries.reshape(N_BLK, SBLK, H, DH)
    grad_all = grad_out.reshape(N_BLK, SBLK, H, DH)
    stat_all = stats.reshape(N_BLK, SBLK, H, 2)
    key_all = jnp.repeat(keys, repeats, axis=1).reshape(N_BLK, SBLK, H, DH)
    value_all = jnp.repeat(values, repeats, axis=1).reshape(N_BLK, SBLK, H, DH)
    positions = (placement.reshape(N_BLK, 2)[:, :, None] * piece_len
                 + jnp.arange(piece_len, dtype=jnp.int32)[None, None, :]).reshape(N_BLK, SBLK).astype(jnp.int32)

    def one_block(shard):
        previous = (shard - 1 + N_BLK) % N_BLK
        first = block_grads(query_all[shard], grad_all[shard], stat_all[shard], key_all[shard], value_all[shard], positions[shard], positions[shard])
        second = block_grads(query_all[shard], grad_all[shard], stat_all[shard], key_all[previous], value_all[previous], positions[shard], positions[previous])
        grad_query = (first[0] + second[0]).astype(jnp.bfloat16)
        return grad_query, first[1], first[2], second[1], second[2]

    grad_query, key_own, value_own, key_next, value_next = lax.map(one_block, jnp.arange(N_BLK, dtype=jnp.int32))
    key_accum = jnp.roll(key_own, 1, axis=0) + key_next
    value_accum = jnp.roll(value_own, 1, axis=0) + value_next
    return (grad_query.reshape(TOKENS, H, DH), key_accum.reshape(TOKENS, H, DH), value_accum.reshape(TOKENS, H, DH))
```

```python
import functools

import jax
import jax.numpy as jnp
from jax import lax
from jax.experimental import pallas as pl
from jax.experimental.pallas import tpu as pltpu
from jax.sharding import PartitionSpec as P

MESH = pl.DeviceIdType.MESH
NT = (((1,), (1,)), ((), ()))
NN = (((1,), (0,)), ((), ()))
TN = (((0,), (0,)), ((), ()))


def dot(a, b, dims):
    return lax.dot_general(a, b, dims, preferred_element_type=jnp.float32)


def kernel(
    place, qin, gin, kvin, sin, dq_out, dk_out, dv_out,
    qbuf, gbuf, sbuf, kvbuf, acc, dqs, dkvs, dkvr,
    q_ss, q_rs, g_ss, g_rs, s_ss, s_rs, kv_ss, kv_rs, x_ss, x_rs, n_ss, n_rs,
    d_ss, d_rs, a_ss, a_rs, l_sem,
):
    f32, bf16 = jnp.float32, jnp.bfloat16
    blk, uly = lax.axis_index("blk"), lax.axis_index("uly")
    plane, half = uly // 2, uly % 2
    row, col = plane // 4, plane % 4
    nxt, prv = (blk + 1) % 32, (blk + 31) % 32
    kv_nxt = (nxt, plane * 2 + (half + (blk + 1) // 32) % 2)
    kv_prv = (prv, plane * 2 + (half + (32 - blk) // 32) % 2)
    factor = 128 ** (-0.5)

    def to(s):
        return ((plane + s % 16) % 16) * 2 + (half + s // 16) % 2

    def frm(s):
        return ((plane + 16 - s % 16) % 16) * 2 + (half + s // 16) % 2

    barrier = pltpu.get_barrier_semaphore()
    for s in range(1, 32):
        pl.semaphore_signal(barrier, inc=1, device_id=(blk, to(s)), device_id_type=MESH)
    for dev in (kv_nxt, kv_prv, (nxt, uly), (prv, uly)):
        pl.semaphore_signal(barrier, inc=1, device_id=dev, device_id_type=MESH)
    pl.semaphore_wait(barrier, 35)

    def remote(src, dst, ss, rs, dev):
        return pltpu.make_async_remote_copy(
            src_ref=src, dst_ref=dst, send_sem=ss, recv_sem=rs, device_id=dev, device_id_type=MESH
        )

    def kv_first(i):
        dest_row = (row + i % 4) % 4
        dest = (dest_row * 4 + col) * 2 + (half + i // 4) % 2
        return remote(
            kvin.at[:, dest_row], kvbuf.at[0, :, row, col, half], kv_ss.at[i], kv_rs.at[i],
            (blk, dest),
        )

    def kv_cols(slot, i):
        dest = (row * 4 + (col + i) % 4) * 2 + half
        return remote(
            kvbuf.at[slot, :, :, col], kvbuf.at[slot, :, :, col],
            x_ss.at[slot * 4 + i], x_rs.at[slot * 4 + i], (blk, dest),
        )

    kv_next = remote(kvbuf.at[0, :, :, col], kvbuf.at[1, :, :, col], n_ss.at[0], n_rs.at[0], kv_nxt)

    def stat_copy(s):
        return remote(sin.at[to(s)], sbuf.at[s], s_ss.at[s], s_rs.at[s], (blk, to(s)))

    def q_copy(s):
        return remote(qin.at[to(s)], qbuf.at[s], q_ss.at[s], q_rs.at[s], (blk, to(s)))

    def g_copy(s):
        return remote(gin.at[to(s)], gbuf.at[s], g_ss.at[s], g_rs.at[s], (blk, to(s)))

    def dq_copy(s):
        return remote(dqs.at[s], dq_out.at[uly], d_ss.at[s], d_rs.at[s], (blk, frm(s)))

    def dq_here(s):
        return remote(dqs.at[s], dq_out.at[to(s)], d_ss.at[s], d_rs.at[s], (blk, to(s)))

    for i in (4, 5, 6, 7, 1, 2, 3):
        kv_first(i).start()
    own_kv = pltpu.make_async_copy(kvin.at[:, row], kvbuf.at[0, :, row, col, half], l_sem.at[0])
    own_kv.start()
    for s in range(16):
        stat_copy(16 + s).start()
        q_copy(16 + s).start()
        g_copy(16 + s).start()
        if s:
            stat_copy(s).start()
            q_copy(s).start()
            g_copy(s).start()
    qbuf[0] = qin[uly]
    gbuf[0] = gin[uly]
    sbuf[0] = sin[uly]
    acc[...] = jnp.zeros_like(acc)

    own_kv.wait()
    for i in (1, 2, 3, 4, 5, 6, 7):
        kv_first(i).wait_recv()
    kv_next.start()
    for i in (1, 2, 3):
        kv_cols(0, i).start()
    kv_next.wait_recv()
    for i in (1, 2, 3):
        kv_cols(1, i).start()
    for slot in (0, 1):
        for i in (1, 2, 3):
            kv_cols(slot, i).wait_recv()

    lane = lax.broadcasted_iota(jnp.int32, (1, 128), 1)
    lane2 = lax.broadcasted_iota(jnp.int32, (2, 128), 1)
    krow = lax.broadcasted_iota(jnp.int32, (512, 1), 0)

    def chunk(c):
        base = 4 * c
        st = jnp.zeros((2, 128), f32)
        for j in range(4):
            st = jnp.where(lane2 // 32 == j, sbuf[base + j], st)
        lse, corr = st[0:1], st[1:2]
        src = ((plane + 16 - (base % 16) - lane // 32) % 16) * 2 + (half + c // 4) % 2
        place_q = jnp.where(src >= 16, place[2 * blk + 1], place[2 * blk])
        qpos = place_q * 512 + (src % 16) * 32 + lane % 32
        q = qbuf[pl.ds(base, 4)].reshape(128, 128)
        g = gbuf[pl.ds(base, 4)].reshape(128, 128)

        def tile(t, dq):
            slot, part = t // 2, t % 2
            kblk = (blk + 32 - slot) % 32
            k = kvbuf[slot, 0, pl.ds(2 * part, 2)].reshape(512, 128)
            v = kvbuf[slot, 1, pl.ds(2 * part, 2)].reshape(512, 128)
            kpos = place[2 * kblk + part] * 512 + krow
            scores = dot(k, q, NT) * factor - lse
            weights = jnp.where(kpos <= qpos, jnp.exp(scores), 0.0)
            dweights = dot(v, g, NT)
            dscores = (weights * (dweights - corr)).astype(bf16)
            acc[t, 1] += dot(weights.astype(bf16), g, NN)
            acc[t, 0] += dot(dscores, q, NN)
            return dq + dot(dscores, k, TN)

        dq = lax.fori_loop(0, 4, tile, jnp.zeros((128, 128), f32))
        dqs[pl.ds(base, 4)] = (dq * factor).astype(bf16).reshape(4, 32, 128)

    def arrive(s):
        stat_copy(s).wait_recv()
        q_copy(s).wait_recv()
        g_copy(s).wait_recv()

    for s in (1, 2, 3):
        arrive(s)
    chunk(0)
    dq_out[uly] = dqs[0]
    for s in (1, 2, 3):
        dq_copy(s).start()

    def step(c, carry):
        for j in range(4):
            arrive(4 * c + j)
        chunk(c)
        for j in range(4):
            dq_copy(4 * c + j).start()
        return carry

    lax.fori_loop(1, 8, step, 0)

    for part in range(2):
        for a in range(2):
            scale = 1.0 if a else factor
            dkvs[a, pl.ds(part * 512, 512)] = (acc[part, a] * scale).astype(bf16)
    accum = [
        remote(dkvs.at[a], dkvr.at[a], a_ss.at[a], a_rs.at[a], (nxt, uly)) for a in range(2)
    ]
    for copy in accum:
        copy.start()
    for a, out in ((0, dk_out), (1, dv_out)):
        accum[a].wait_recv()
        for part in range(2):
            scale = 1.0 if a else factor
            rows = pl.ds(part * 512, 512)
            out[rows] = acc[2 + part, a] * scale + dkvr[a, rows].astype(f32)

    def drain(s, carry):
        dq_here(s).wait_recv()
        dq_copy(s).wait_send()
        stat_copy(s).wait_send()
        q_copy(s).wait_send()
        g_copy(s).wait_send()
        return carry

    lax.fori_loop(1, 32, drain, 0)
    for i in range(1, 8):
        kv_first(i).wait_send()
    kv_next.wait_send()
    for slot in (0, 1):
        for i in (1, 2, 3):
            kv_cols(slot, i).wait_send()
    for copy in accum:
        copy.wait_send()


def per_device(queries, keys, values, grad_out, stats, placement):
    f32, bf16 = jnp.float32, jnp.bfloat16
    q_heads = queries.transpose(1, 0, 2)
    g_heads = grad_out.transpose(1, 0, 2)
    kv_heads = jnp.stack([keys.transpose(1, 0, 2), values.transpose(1, 0, 2)])
    stat_rows = jnp.tile(stats.transpose(1, 2, 0).astype(f32), (1, 1, 4))
    vmem = pl.BlockSpec(memory_space=pltpu.VMEM)
    sem = pltpu.SemaphoreType.DMA
    dq, dk, dv = pl.pallas_call(
        kernel,
        name="exchange_grads",
        out_shape=(
            jax.ShapeDtypeStruct((32, 32, 128), bf16),
            jax.ShapeDtypeStruct((1024, 128), f32),
            jax.ShapeDtypeStruct((1024, 128), f32),
        ),
        in_specs=[pl.BlockSpec(memory_space=pltpu.SMEM)] + [vmem] * 4,
        out_specs=(vmem, vmem, vmem),
        scratch_shapes=[
            pltpu.VMEM((32, 32, 128), bf16),
            pltpu.VMEM((32, 32, 128), bf16),
            pltpu.VMEM((32, 2, 128), f32),
            pltpu.VMEM((2, 2, 4, 4, 2, 32, 128), bf16),
            pltpu.VMEM((4, 2, 512, 128), f32),
            pltpu.VMEM((32, 32, 128), bf16),
            pltpu.VMEM((2, 1024, 128), bf16),
            pltpu.VMEM((2, 1024, 128), bf16),
            sem((32,)), sem((32,)), sem((32,)), sem((32,)), sem((32,)), sem((32,)),
            sem((8,)), sem((8,)), sem((8,)), sem((8,)), sem((1,)), sem((1,)),
            sem((32,)), sem((32,)), sem((2,)), sem((2,)), sem((1,)),
        ],
        compiler_params=pltpu.CompilerParams(collective_id=0, has_side_effects=True),
    )(placement, q_heads, g_heads, kv_heads, stat_rows)
    return dq.transpose(1, 0, 2), dk[:, None, :], dv[:, None, :]


def solution(mesh):
    tokens = P(("blk", "uly"), None, None)
    return jax.shard_map(
        per_device,
        mesh=mesh,
        in_specs=(tokens,) * 5 + (P(),),
        out_specs=(tokens, P("blk", "uly", None), P("blk", "uly", None)),
        check_vma=False,
    )
```

```python
import jax
import jax.numpy as jnp
from jax import lax
from jax.experimental import pallas as pl
from jax.experimental.pallas import tpu as pltpu
from jax.sharding import PartitionSpec as P

MESH = pl.DeviceIdType.MESH
NT = (((1,), (1,)), ((), ()))
NN = (((1,), (0,)), ((), ()))
TN = (((0,), (0,)), ((), ()))


def dot(a, b, dims):
    return lax.dot_general(a, b, dims, preferred_element_type=jnp.float32)


def kernel(
    place, qin, gin, kin, vin, sin, dq_out, dk_out, dv_out,
    qgs, qgbuf, kvin, sbuf, kvbuf, acc, dqs, dkvs, dkvr,
    q_ss, q_rs, s_ss, s_rs, kv_ss, kv_rs, x_ss, x_rs, n_ss, n_rs,
    d_ss, d_rs, a_ss, a_rs, l_sem,
):
    f32, bf16 = jnp.float32, jnp.bfloat16
    blk, uly = lax.axis_index("blk"), lax.axis_index("uly")
    plane, half = uly // 2, uly % 2
    row, col = plane // 4, plane % 4
    nxt, prv = (blk + 1) % 32, (blk + 31) % 32
    kv_nxt = (nxt, plane * 2 + (half + (blk + 1) // 32) % 2)
    kv_prv = (prv, plane * 2 + (half + (32 - blk) // 32) % 2)
    factor = 128 ** (-0.5)

    def to(s):
        return ((plane + s % 16) % 16) * 2 + (half + s // 16) % 2

    def frm(s):
        return ((plane + 16 - s % 16) % 16) * 2 + (half + s // 16) % 2

    barrier = pltpu.get_barrier_semaphore()
    for s in range(1, 32):
        pl.semaphore_signal(barrier, inc=1, device_id=(blk, to(s)), device_id_type=MESH)
    for dev in (kv_nxt, kv_prv, (nxt, uly), (prv, uly)):
        pl.semaphore_signal(barrier, inc=1, device_id=dev, device_id_type=MESH)
    kvin[0] = kin[...].transpose(1, 0, 2)
    kvin[1] = vin[...].transpose(1, 0, 2)
    qgs[:, 0] = qin[...].transpose(1, 0, 2)
    qgs[:, 1] = gin[...].transpose(1, 0, 2)
    acc[...] = jnp.zeros_like(acc)
    pl.semaphore_wait(barrier, 35)

    def remote(src, dst, ss, rs, dev):
        return pltpu.make_async_remote_copy(
            src_ref=src, dst_ref=dst, send_sem=ss, recv_sem=rs, device_id=dev, device_id_type=MESH
        )

    def kv_first(i):
        dest_row = (row + i % 4) % 4
        dest = (dest_row * 4 + col) * 2 + (half + i // 4) % 2
        return remote(
            kvin.at[:, dest_row], kvbuf.at[0, :, row, col, half], kv_ss.at[i], kv_rs.at[i],
            (blk, dest),
        )

    def kv_cols(slot, i):
        dest = (row * 4 + (col + i) % 4) * 2 + half
        return remote(
            kvbuf.at[slot, :, :, col], kvbuf.at[slot, :, :, col],
            x_ss.at[slot * 4 + i], x_rs.at[slot * 4 + i], (blk, dest),
        )

    kv_next = remote(kvbuf.at[0, :, :, col], kvbuf.at[1, :, :, col], n_ss.at[0], n_rs.at[0], kv_nxt)

    def stat_copy(s):
        return remote(sin.at[to(s)], sbuf.at[s], s_ss.at[s], s_rs.at[s], (blk, to(s)))

    def qg_copy(s):
        return remote(qgs.at[to(s)], qgbuf.at[s], q_ss.at[s], q_rs.at[s], (blk, to(s)))

    def dq_copy(s):
        return remote(dqs.at[s], dq_out.at[uly], d_ss.at[s], d_rs.at[s], (blk, frm(s)))

    def dq_here(s):
        return remote(dqs.at[s], dq_out.at[to(s)], d_ss.at[s], d_rs.at[s], (blk, to(s)))

    for i in (4, 5, 6, 7, 1, 2, 3):
        kv_first(i).start()
    own_kv = pltpu.make_async_copy(kvin.at[:, row], kvbuf.at[0, :, row, col, half], l_sem.at[0])
    own_kv.start()
    def send(lo, hi):
        for s in range(lo, hi):
            stat_copy(s).start()
            qg_copy(s).start()

    send(16, 20)
    send(1, 16)
    qgbuf[0] = qgs[uly]
    sbuf[0] = sin[uly]

    own_kv.wait()
    for i in (1, 2, 3, 4, 5, 6, 7):
        kv_first(i).wait_recv()
    kv_next.start()
    for i in (1, 2, 3):
        kv_cols(0, i).start()
    send(20, 24)
    kv_next.wait_recv()
    for i in (1, 2, 3):
        kv_cols(1, i).start()
    send(24, 32)
    for slot in (0, 1):
        for i in (1, 2, 3):
            kv_cols(slot, i).wait_recv()

    lane = lax.broadcasted_iota(jnp.int32, (1, 128), 1)
    lane2 = lax.broadcasted_iota(jnp.int32, (2, 128), 1)
    krow = lax.broadcasted_iota(jnp.int32, (512, 1), 0)

    def chunk(c):
        base = 4 * c
        st = jnp.zeros((2, 128), f32)
        for j in range(4):
            st = jnp.where(lane2 // 32 == j, sbuf[base + j], st)
        lse, corr = st[0:1], st[1:2]
        src = ((plane + 16 - (base % 16) - lane // 32) % 16) * 2 + (half + c // 4) % 2
        place_q = jnp.where(src >= 16, place[2 * blk + 1], place[2 * blk])
        qpos = place_q * 512 + (src % 16) * 32 + lane % 32
        q = qgbuf[pl.ds(base, 4), 0].reshape(128, 128)
        g = qgbuf[pl.ds(base, 4), 1].reshape(128, 128)

        def tile(t, dq):
            slot, part = t // 2, t % 2
            kblk = (blk + 32 - slot) % 32
            k = kvbuf[slot, 0, pl.ds(2 * part, 2)].reshape(512, 128)
            v = kvbuf[slot, 1, pl.ds(2 * part, 2)].reshape(512, 128)
            kpos = place[2 * kblk + part] * 512 + krow
            scores = dot(k, q, NT) * factor - lse
            weights = jnp.where(kpos <= qpos, jnp.exp(scores), 0.0)
            dweights = dot(v, g, NT)
            dscores = (weights * (dweights - corr)).astype(bf16)
            acc[t, 1] += dot(weights.astype(bf16), g, NN)
            acc[t, 0] += dot(dscores, q, NN)
            return dq + dot(dscores, k, TN)

        dq = lax.fori_loop(0, 4, tile, jnp.zeros((128, 128), f32))
        dqs[pl.ds(base, 4)] = (dq * factor).astype(bf16).reshape(4, 32, 128)

    def arrive(s):
        stat_copy(s).wait_recv()
        qg_copy(s).wait_recv()

    for s in (1, 2, 3):
        arrive(s)
    chunk(0)
    dq_out[uly] = dqs[0]
    for s in (1, 2, 3):
        dq_copy(s).start()

    def step(c, carry):
        for j in range(4):
            arrive(4 * c + j)
        chunk(c)
        for j in range(4):
            dq_copy(4 * c + j).start()
        return carry

    lax.fori_loop(1, 8, step, 0)

    for part in range(2):
        for a in range(2):
            scale = 1.0 if a else factor
            dkvs[a, pl.ds(part * 512, 512)] = (acc[part, a] * scale).astype(bf16)
    accum = [
        remote(dkvs.at[a], dkvr.at[a], a_ss.at[a], a_rs.at[a], (nxt, uly)) for a in range(2)
    ]
    for copy in accum:
        copy.start()
    for a, out in ((0, dk_out), (1, dv_out)):
        accum[a].wait_recv()
        for part in range(2):
            scale = 1.0 if a else factor
            rows = pl.ds(part * 512, 512)
            out[rows] = acc[2 + part, a] * scale + dkvr[a, rows].astype(f32)

    def drain(s, carry):
        dq_here(s).wait_recv()
        dq_copy(s).wait_send()
        stat_copy(s).wait_send()
        qg_copy(s).wait_send()
        return carry

    lax.fori_loop(1, 32, drain, 0)
    for i in range(1, 8):
        kv_first(i).wait_send()
    kv_next.wait_send()
    for slot in (0, 1):
        for i in (1, 2, 3):
            kv_cols(slot, i).wait_send()
    for copy in accum:
        copy.wait_send()


def per_device(queries, keys, values, grad_out, stats, placement):
    f32, bf16 = jnp.float32, jnp.bfloat16
    stat_rows = jnp.tile(stats.transpose(1, 2, 0).astype(f32), (1, 1, 4))
    vmem = pl.BlockSpec(memory_space=pltpu.VMEM)
    sem = pltpu.SemaphoreType.DMA
    dq, dk, dv = pl.pallas_call(
        kernel,
        name="exchange_grads",
        out_shape=(
            jax.ShapeDtypeStruct((32, 32, 128), bf16),
            jax.ShapeDtypeStruct((1024, 128), f32),
            jax.ShapeDtypeStruct((1024, 128), f32),
        ),
        in_specs=[pl.BlockSpec(memory_space=pltpu.SMEM)] + [vmem] * 5,
        out_specs=(vmem, vmem, vmem),
        scratch_shapes=[
            pltpu.VMEM((32, 2, 32, 128), bf16),
            pltpu.VMEM((32, 2, 32, 128), bf16),
            pltpu.VMEM((2, 4, 32, 128), bf16),
            pltpu.VMEM((32, 2, 128), f32),
            pltpu.VMEM((2, 2, 4, 4, 2, 32, 128), bf16),
            pltpu.VMEM((4, 2, 512, 128), f32),
            pltpu.VMEM((32, 32, 128), bf16),
            pltpu.VMEM((2, 1024, 128), bf16),
            pltpu.VMEM((2, 1024, 128), bf16),
            sem((32,)), sem((32,)), sem((32,)), sem((32,)),
            sem((8,)), sem((8,)), sem((8,)), sem((8,)), sem((1,)), sem((1,)),
            sem((32,)), sem((32,)), sem((2,)), sem((2,)), sem((1,)),
        ],
        compiler_params=pltpu.CompilerParams(collective_id=0, has_side_effects=True),
    )(placement, queries, grad_out, keys, values, stat_rows)
    return dq.transpose(1, 0, 2), dk[:, None, :], dv[:, None, :]


def solution(mesh):
    tokens = P(("blk", "uly"), None, None)
    return jax.shard_map(
        per_device,
        mesh=mesh,
        in_specs=(tokens,) * 5 + (P(),),
        out_specs=(tokens, P("blk", "uly", None), P("blk", "uly", None)),
        check_vma=False,
    )
```

```python
import jax
import jax.numpy as jnp
from jax import lax
from jax.experimental import pallas as pl
from jax.experimental.pallas import tpu as pltpu
from jax.sharding import PartitionSpec as P

MESH = pl.DeviceIdType.MESH
NT = (((1,), (1,)), ((), ()))
NN = (((1,), (0,)), ((), ()))
TN = (((0,), (0,)), ((), ()))


def dot(a, b, dims):
    return lax.dot_general(a, b, dims, preferred_element_type=jnp.float32)


def kernel(
    place, qin, gin, kin, vin, sin, dq_out, dk_out, dv_out,
    qgs, inbuf, crossbuf, kvin, sinbuf, scross, kvbuf, acc, dqs, dqx, dkvs, dkvr,
    q_ss, q_rs, s_ss, s_rs, c_ss, c_rs, t_ss, t_rs, kv_ss, kv_rs, x_ss, x_rs, n_ss, n_rs,
    d_ss, d_rs, y_ss, y_rs, f_ss, f_rs, a_ss, a_rs, l_sem,
):
    f32, bf16 = jnp.float32, jnp.bfloat16
    blk, uly = lax.axis_index("blk"), lax.axis_index("uly")
    plane, half = uly // 2, uly % 2
    row, col = plane // 4, plane % 4
    nxt, prv = (blk + 1) % 32, (blk + 31) % 32
    kv_nxt = (nxt, plane * 2 + (half + (blk + 1) // 32) % 2)
    kv_prv = (prv, plane * 2 + (half + (32 - blk) // 32) % 2)
    factor = 128 ** (-0.5)

    def to(s):
        return ((plane + s % 16) % 16) * 2 + (half + s // 16) % 2

    def frm(s):
        return ((plane + 16 - s % 16) % 16) * 2 + (half + s // 16) % 2

    barrier = pltpu.get_barrier_semaphore()
    for s in tuple(range(1, 17)) + (20, 24, 28):
        pl.semaphore_signal(barrier, inc=1, device_id=(blk, to(s)), device_id_type=MESH)
    for dev in (kv_nxt, kv_prv, (nxt, uly), (prv, uly)):
        pl.semaphore_signal(barrier, inc=1, device_id=dev, device_id_type=MESH)
    kvin[0] = kin[...].transpose(1, 0, 2)
    kvin[1] = vin[...].transpose(1, 0, 2)
    qgs[:, 0] = qin[...].transpose(1, 0, 2)
    qgs[:, 1] = gin[...].transpose(1, 0, 2)
    acc[...] = jnp.zeros_like(acc)
    pl.semaphore_wait(barrier, 23)

    def remote(src, dst, ss, rs, dev):
        return pltpu.make_async_remote_copy(
            src_ref=src, dst_ref=dst, send_sem=ss, recv_sem=rs, device_id=dev, device_id_type=MESH
        )

    def kv_first(i):
        dest_row = (row + i % 4) % 4
        dest = (dest_row * 4 + col) * 2 + (half + i // 4) % 2
        return remote(
            kvin.at[:, dest_row], kvbuf.at[0, :, row, col, half], kv_ss.at[i], kv_rs.at[i],
            (blk, dest),
        )

    def kv_cols(slot, i):
        dest = (row * 4 + (col + i) % 4) * 2 + half
        return remote(
            kvbuf.at[slot, :, :, col], kvbuf.at[slot, :, :, col],
            x_ss.at[slot * 4 + i], x_rs.at[slot * 4 + i], (blk, dest),
        )

    kv_next = remote(kvbuf.at[0, :, :, col], kvbuf.at[1, :, :, col], n_ss.at[0], n_rs.at[0], kv_nxt)

    far = plane * 2 + (half + 1) % 2

    def pair(r):
        return pl.ds(((plane + r) % 16) * 2, 2)

    def stat_plane(r):
        return remote(sin.at[pair(r)], sinbuf.at[:, r], s_ss.at[r], s_rs.at[r], (blk, to(r)))

    def qg_plane(r):
        return remote(qgs.at[pair(r)], inbuf.at[:, r], q_ss.at[r], q_rs.at[r], (blk, to(r)))

    def stat_cross(c):
        rows = pl.ds(4 * c, 4)
        return remote(
            sinbuf.at[1 - half, rows], scross.at[rows], t_ss.at[c], t_rs.at[c], (blk, far)
        )

    def qg_cross(c):
        rows = pl.ds(4 * c, 4)
        return remote(
            inbuf.at[1 - half, rows], crossbuf.at[rows], c_ss.at[c], c_rs.at[c], (blk, far)
        )

    def dq_plane(r):
        return remote(dqs.at[r], dq_out.at[uly], d_ss.at[r], d_rs.at[r], (blk, frm(r)))

    def dq_here(r):
        return remote(dqs.at[r], dq_out.at[to(r)], d_ss.at[r], d_rs.at[r], (blk, to(r)))

    def dq_cross(c):
        rows = pl.ds(4 * c, 4)
        return remote(
            dqs.at[pl.ds(16 + 4 * c, 4)], dqx.at[rows], y_ss.at[c], y_rs.at[c], (blk, far)
        )

    def dq_pass(r):
        return remote(dqx.at[r], dq_out.at[far], f_ss.at[r], f_rs.at[r], (blk, frm(r)))

    def dq_passed(r):
        head = ((plane + r) % 16) * 2 + 1 - half
        return remote(dqx.at[r], dq_out.at[head], f_ss.at[r], f_rs.at[r], (blk, to(r)))

    for i in (4, 5, 6, 7, 1, 2, 3):
        kv_first(i).start()
    own_kv = pltpu.make_async_copy(kvin.at[:, row], kvbuf.at[0, :, row, col, half], l_sem.at[0])
    own_kv.start()
    own_qg = pltpu.make_async_copy(qgs.at[pair(0)], inbuf.at[:, 0], l_sem.at[1])
    own_qg.start()
    own_stat = pltpu.make_async_copy(sin.at[pair(0)], sinbuf.at[:, 0], l_sem.at[2])
    own_stat.start()
    for r in range(1, 16):
        stat_plane(r).start()
        qg_plane(r).start()

    def cross(c):
        if c == 0:
            own_qg.wait()
            own_stat.wait()
        for r in range(max(1, 4 * c), 4 * c + 4):
            stat_plane(r).wait_recv()
            qg_plane(r).wait_recv()
        stat_cross(c).start()
        qg_cross(c).start()

    cross(0)
    cross(1)
    own_kv.wait()
    for i in (1, 2, 3, 4, 5, 6, 7):
        kv_first(i).wait_recv()
    kv_next.start()
    for i in (1, 2, 3):
        kv_cols(0, i).start()
    cross(2)
    kv_next.wait_recv()
    for i in (1, 2, 3):
        kv_cols(1, i).start()
    cross(3)
    for slot in (0, 1):
        for i in (1, 2, 3):
            kv_cols(slot, i).wait_recv()

    lane = lax.broadcasted_iota(jnp.int32, (1, 128), 1)
    krow = lax.broadcasted_iota(jnp.int32, (1024, 1), 0)

    def chunk(c, stats, qg):
        base = 4 * c
        lse = corr = jnp.zeros((1, 128), f32)
        for j in range(4):
            here = stats(j)
            turned = pltpu.roll(here, 32, 1)
            first, second = (here, turned) if j % 2 == 0 else (turned, here)
            lse = jnp.where(lane // 32 == j, first, lse)
            corr = jnp.where(lane // 32 == j, second, corr)
        src = ((plane + 16 - (base % 16) - lane // 32) % 16) * 2 + (half + c // 4) % 2
        place_q = jnp.where(src >= 16, place[2 * blk + 1], place[2 * blk])
        qpos = place_q * 512 + (src % 16) * 32 + lane % 32
        q, g = qg(0).reshape(128, 128), qg(1).reshape(128, 128)

        def tile(slot, dq):
            kblk = (blk + 32 - slot) % 32
            k = kvbuf[slot, 0].reshape(1024, 128)
            v = kvbuf[slot, 1].reshape(1024, 128)
            place_k = jnp.where(krow >= 512, place[2 * kblk + 1], place[2 * kblk])
            kpos = place_k * 512 + krow % 512
            scores = dot(k, q, NT) * factor - lse
            weights = jnp.where(kpos <= qpos, jnp.exp(scores), 0.0)
            dweights = dot(v, g, NT)
            dscores = (weights * (dweights - corr)).astype(bf16)
            acc[slot, 1] += dot(weights.astype(bf16), g, NN)
            acc[slot, 0] += dot(dscores, q, NN)
            return dq + dot(dscores, k, TN)

        dq = lax.fori_loop(0, 2, tile, jnp.zeros((128, 128), f32))
        dqs[pl.ds(base, 4)] = (dq * factor).astype(bf16).reshape(4, 32, 128)

    def near_chunk(c):
        chunk(
            c,
            lambda j: sinbuf[half, 4 * c + j],
            lambda a: inbuf[half, pl.ds(4 * c, 4), a],
        )

    near_chunk(0)
    dq_out[uly] = dqs[0]
    for r in (1, 2, 3):
        dq_plane(r).start()

    def near(c, carry):
        near_chunk(c)
        for j in range(4):
            dq_plane(4 * c + j).start()
        return carry

    lax.fori_loop(1, 4, near, 0)

    def distant(c, carry):
        stat_cross(c).wait_recv()
        qg_cross(c).wait_recv()
        chunk(
            c + 4,
            lambda j: scross[4 * c + j],
            lambda a: crossbuf[pl.ds(4 * c, 4), a],
        )
        dq_cross(c).start()
        return carry

    lax.fori_loop(0, 4, distant, 0)

    dkvs[0] = (acc[0, 0] * factor).astype(bf16)
    dkvs[1] = acc[0, 1].astype(bf16)
    accum = [
        remote(dkvs.at[a], dkvr.at[a], a_ss.at[a], a_rs.at[a], (nxt, uly)) for a in range(2)
    ]
    for copy in accum:
        copy.start()
    dq_cross(0).wait_recv()
    dq_out[far] = dqx[0]
    for r in (1, 2, 3):
        dq_pass(r).start()

    def onward(c, carry):
        dq_cross(c).wait_recv()
        for j in range(4):
            dq_pass(4 * c + j).start()
        return carry

    lax.fori_loop(1, 4, onward, 0)
    for a, out in ((0, dk_out), (1, dv_out)):
        accum[a].wait_recv()
        out[...] = acc[1, a] * (1.0 if a else factor) + dkvr[a].astype(f32)

    def drain(r, carry):
        dq_here(r).wait_recv()
        dq_passed(r).wait_recv()
        dq_plane(r).wait_send()
        dq_pass(r).wait_send()
        stat_plane(r).wait_send()
        qg_plane(r).wait_send()
        return carry

    lax.fori_loop(1, 16, drain, 0)
    for c in range(4):
        stat_cross(c).wait_send()
        qg_cross(c).wait_send()
        dq_cross(c).wait_send()
    for i in range(1, 8):
        kv_first(i).wait_send()
    kv_next.wait_send()
    for slot in (0, 1):
        for i in (1, 2, 3):
            kv_cols(slot, i).wait_send()
    for copy in accum:
        copy.wait_send()


def per_device(queries, keys, values, grad_out, stats, placement):
    f32, bf16 = jnp.float32, jnp.bfloat16
    stat_rows = jnp.tile(stats.transpose(1, 2, 0).astype(f32).reshape(32, 1, 64), (1, 1, 2))
    vmem = pl.BlockSpec(memory_space=pltpu.VMEM)
    sem = pltpu.SemaphoreType.DMA
    dq, dk, dv = pl.pallas_call(
        kernel,
        name="exchange_grads",
        out_shape=(
            jax.ShapeDtypeStruct((32, 32, 128), bf16),
            jax.ShapeDtypeStruct((1024, 128), f32),
            jax.ShapeDtypeStruct((1024, 128), f32),
        ),
        in_specs=[pl.BlockSpec(memory_space=pltpu.SMEM)] + [vmem] * 5,
        out_specs=(vmem, vmem, vmem),
        scratch_shapes=[
            pltpu.VMEM((32, 2, 32, 128), bf16),
            pltpu.VMEM((2, 16, 2, 32, 128), bf16),
            pltpu.VMEM((16, 2, 32, 128), bf16),
            pltpu.VMEM((2, 4, 32, 128), bf16),
            pltpu.VMEM((2, 16, 1, 128), f32),
            pltpu.VMEM((16, 1, 128), f32),
            pltpu.VMEM((2, 2, 4, 4, 2, 32, 128), bf16),
            pltpu.VMEM((2, 2, 1024, 128), f32),
            pltpu.VMEM((32, 32, 128), bf16),
            pltpu.VMEM((16, 32, 128), bf16),
            pltpu.VMEM((2, 1024, 128), bf16),
            pltpu.VMEM((2, 1024, 128), bf16),
            sem((16,)), sem((16,)), sem((16,)), sem((16,)), sem((4,)), sem((4,)), sem((4,)), sem((4,)),
            sem((8,)), sem((8,)), sem((8,)), sem((8,)), sem((1,)), sem((1,)),
            sem((16,)), sem((16,)), sem((4,)), sem((4,)), sem((16,)), sem((16,)),
            sem((2,)), sem((2,)), sem((3,)),
        ],
        compiler_params=pltpu.CompilerParams(collective_id=0, has_side_effects=True),
    )(placement, queries, grad_out, keys, values, stat_rows)
    return dq.transpose(1, 0, 2), dk[:, None, :], dv[:, None, :]


def solution(mesh):
    tokens = P(("blk", "uly"), None, None)
    return jax.shard_map(
        per_device,
        mesh=mesh,
        in_specs=(tokens,) * 5 + (P(),),
        out_specs=(tokens, P("blk", "uly", None), P("blk", "uly", None)),
        check_vma=False,
    )
```

```python
import jax
import jax.numpy as jnp
from jax import lax
from jax.experimental import pallas as pl
from jax.experimental.pallas import tpu as pltpu
from jax.sharding import PartitionSpec as P

MESH = pl.DeviceIdType.MESH
NT = (((1,), (1,)), ((), ()))
NN = (((1,), (0,)), ((), ()))
TN = (((0,), (0,)), ((), ()))


def dot(a, b, dims):
    return lax.dot_general(a, b, dims, preferred_element_type=jnp.float32)


def kernel(
    place, qin, gin, kin, vin, stin, dq_out, dk_out, dv_out,
    qgs, inbuf, crossbuf, kvin, sin, sinbuf, scross, kvbuf, acc, dqs, dqx, dkvs, dkvr,
    q_ss, q_rs, s_ss, s_rs, c_ss, c_rs, t_ss, t_rs, kv_ss, kv_rs, x_ss, x_rs, n_ss, n_rs,
    d_ss, d_rs, y_ss, y_rs, f_ss, f_rs, a_ss, a_rs, l_sem,
):
    f32, bf16 = jnp.float32, jnp.bfloat16
    blk, uly = lax.axis_index("blk"), lax.axis_index("uly")
    plane, half = uly // 2, uly % 2
    row, col = plane // 4, plane % 4
    nxt, prv = (blk + 1) % 32, (blk + 31) % 32
    kv_nxt = (nxt, plane * 2 + (half + (blk + 1) // 32) % 2)
    kv_prv = (prv, plane * 2 + (half + (32 - blk) // 32) % 2)
    factor = 128 ** (-0.5)

    def to(s):
        return ((plane + s % 16) % 16) * 2 + (half + s // 16) % 2

    def frm(s):
        return ((plane + 16 - s % 16) % 16) * 2 + (half + s // 16) % 2

    barrier = pltpu.get_barrier_semaphore()
    for s in tuple(range(1, 17)) + (20, 24, 28):
        pl.semaphore_signal(barrier, inc=1, device_id=(blk, to(s)), device_id_type=MESH)
    for dev in (kv_nxt, kv_prv, (nxt, uly), (prv, uly)):
        pl.semaphore_signal(barrier, inc=1, device_id=dev, device_id_type=MESH)
    kvin[0] = kin[...].transpose(1, 0, 2)
    kvin[1] = vin[...].transpose(1, 0, 2)

    def by_head():
        both = stin[...].astype(f32)
        log_norm, correction = both[:, 0, :], both[:, 1, :]
        lanes = [log_norm, correction, log_norm, correction]
        sin[:, 0, :] = jnp.concatenate(lanes, axis=1)
        qgs[:, 0] = qin[...].transpose(1, 0, 2)
        qgs[:, 1] = gin[...].transpose(1, 0, 2)

    pl.when(half == 0)(by_head)
    pl.semaphore_wait(barrier, 23)

    def remote(src, dst, ss, rs, dev):
        return pltpu.make_async_remote_copy(
            src_ref=src, dst_ref=dst, send_sem=ss, recv_sem=rs, device_id=dev, device_id_type=MESH
        )

    def kv_first(i):
        dest_row = (row + i % 4) % 4
        dest = (dest_row * 4 + col) * 2 + (half + i // 4) % 2
        return remote(
            kvin.at[:, dest_row], kvbuf.at[0, :, row, col, half], kv_ss.at[i], kv_rs.at[i],
            (blk, dest),
        )

    def kv_cols(slot, i):
        dest = (row * 4 + (col + i) % 4) * 2 + half
        return remote(
            kvbuf.at[slot, :, :, col], kvbuf.at[slot, :, :, col],
            x_ss.at[slot * 4 + i], x_rs.at[slot * 4 + i], (blk, dest),
        )

    kv_next = remote(kvbuf.at[0, :, :, col], kvbuf.at[1, :, :, col], n_ss.at[0], n_rs.at[0], kv_nxt)

    far = plane * 2 + (half + 1) % 2

    def pair(r):
        return pl.ds(((plane + r) % 16) * 2, 2)

    def stat_plane(r):
        return remote(sin.at[pair(r)], sinbuf.at[:, r], s_ss.at[r], s_rs.at[r], (blk, to(r)))

    def qg_plane(r):
        return remote(qgs.at[pair(r)], inbuf.at[:, r], q_ss.at[r], q_rs.at[r], (blk, to(r)))

    def stat_cross(c):
        rows = pl.ds(4 * c, 4)
        return remote(
            sinbuf.at[1 - half, rows], scross.at[rows], t_ss.at[c], t_rs.at[c], (blk, far)
        )

    def qg_cross(c):
        rows = pl.ds(4 * c, 4)
        return remote(
            inbuf.at[1 - half, rows], crossbuf.at[rows], c_ss.at[c], c_rs.at[c], (blk, far)
        )

    def dq_plane(r):
        return remote(dqs.at[r], dq_out.at[uly], d_ss.at[r], d_rs.at[r], (blk, frm(r)))

    def dq_here(r):
        return remote(dqs.at[r], dq_out.at[to(r)], d_ss.at[r], d_rs.at[r], (blk, to(r)))

    def dq_cross(c):
        rows = pl.ds(4 * c, 4)
        return remote(
            dqs.at[pl.ds(16 + 4 * c, 4)], dqx.at[rows], y_ss.at[c], y_rs.at[c], (blk, far)
        )

    def dq_pass(r):
        return remote(dqx.at[r], dq_out.at[far], f_ss.at[r], f_rs.at[r], (blk, frm(r)))

    def dq_passed(r):
        head = ((plane + r) % 16) * 2 + 1 - half
        return remote(dqx.at[r], dq_out.at[head], f_ss.at[r], f_rs.at[r], (blk, to(r)))

    for i in (4, 5, 6, 7, 1, 2, 3):
        kv_first(i).start()
    own_kv = pltpu.make_async_copy(kvin.at[:, row], kvbuf.at[0, :, row, col, half], l_sem.at[0])
    own_kv.start()
    pl.when(half == 1)(by_head)
    own_qg = pltpu.make_async_copy(qgs.at[pair(0)], inbuf.at[:, 0], l_sem.at[1])
    own_qg.start()
    own_stat = pltpu.make_async_copy(sin.at[pair(0)], sinbuf.at[:, 0], l_sem.at[2])
    own_stat.start()
    for r in range(1, 16):
        stat_plane(r).start()
        qg_plane(r).start()

    acc[...] = jnp.zeros_like(acc)

    def cross(c):
        if c == 0:
            own_qg.wait()
            own_stat.wait()
        for r in range(max(1, 4 * c), 4 * c + 4):
            stat_plane(r).wait_recv()
            qg_plane(r).wait_recv()
        stat_cross(c).start()
        qg_cross(c).start()

    cross(0)
    cross(1)
    own_kv.wait()
    for i in (1, 2, 3, 4, 5, 6, 7):
        kv_first(i).wait_recv()
    kv_next.start()
    for i in (1, 2, 3):
        kv_cols(0, i).start()
    cross(2)
    kv_next.wait_recv()
    for i in (1, 2, 3):
        kv_cols(1, i).start()
    cross(3)
    for slot in (0, 1):
        for i in (1, 2, 3):
            kv_cols(slot, i).wait_recv()

    lane = lax.broadcasted_iota(jnp.int32, (1, 128), 1)
    krow = lax.broadcasted_iota(jnp.int32, (1024, 1), 0)

    def chunk(c, stats, qg):
        base = 4 * c
        lse = corr = jnp.zeros((1, 128), f32)
        for j in range(4):
            here = stats(j)
            turned = pltpu.roll(here, 32, 1)
            first, second = (here, turned) if j % 2 == 0 else (turned, here)
            lse = jnp.where(lane // 32 == j, first, lse)
            corr = jnp.where(lane // 32 == j, second, corr)
        src = ((plane + 16 - (base % 16) - lane // 32) % 16) * 2 + (half + c // 4) % 2
        place_q = jnp.where(src >= 16, place[2 * blk + 1], place[2 * blk])
        qpos = place_q * 512 + (src % 16) * 32 + lane % 32
        q, g = qg(0).reshape(128, 128), qg(1).reshape(128, 128)

        def tile(slot, dq):
            kblk = (blk + 32 - slot) % 32
            k = kvbuf[slot, 0].reshape(1024, 128)
            v = kvbuf[slot, 1].reshape(1024, 128)
            place_k = jnp.where(krow >= 512, place[2 * kblk + 1], place[2 * kblk])
            kpos = place_k * 512 + krow % 512
            scores = dot(k, q, NT) * factor - lse
            weights = jnp.where(kpos <= qpos, jnp.exp(scores), 0.0)
            dweights = dot(v, g, NT)
            dscores = (weights * (dweights - corr)).astype(bf16)
            acc[slot, 1] += dot(weights.astype(bf16), g, NN)
            acc[slot, 0] += dot(dscores, q, NN)
            return dq + dot(dscores, k, TN)

        dq = lax.fori_loop(0, 2, tile, jnp.zeros((128, 128), f32))
        dqs[pl.ds(base, 4)] = (dq * factor).astype(bf16).reshape(4, 32, 128)

    def near_chunk(c):
        chunk(
            c,
            lambda j: sinbuf[half, 4 * c + j],
            lambda a: inbuf[half, pl.ds(4 * c, 4), a],
        )

    near_chunk(0)
    dq_out[uly] = dqs[0]
    for r in (1, 2, 3):
        dq_plane(r).start()

    def near(c, carry):
        near_chunk(c)
        for j in range(4):
            dq_plane(4 * c + j).start()
        return carry

    lax.fori_loop(1, 4, near, 0)

    def distant_chunk(c):
        stat_cross(c).wait_recv()
        qg_cross(c).wait_recv()
        chunk(
            c + 4,
            lambda j: scross[4 * c + j],
            lambda a: crossbuf[pl.ds(4 * c, 4), a],
        )

    def distant(c, carry):
        distant_chunk(c)
        dq_cross(c).start()
        return carry

    lax.fori_loop(0, 3, distant, 0)
    distant_chunk(3)
    dkvs[0] = (acc[0, 0] * factor).astype(bf16)
    dkvs[1] = acc[0, 1].astype(bf16)
    accum = [
        remote(dkvs.at[a], dkvr.at[a], a_ss.at[a], a_rs.at[a], (nxt, uly)) for a in range(2)
    ]
    for copy in accum:
        copy.start()
    dq_cross(3).start()
    dq_cross(0).wait_recv()
    dq_out[far] = dqx[0]
    for r in (1, 2, 3):
        dq_pass(r).start()

    def onward(c, carry):
        dq_cross(c).wait_recv()
        for j in range(4):
            dq_pass(4 * c + j).start()
        return carry

    lax.fori_loop(1, 4, onward, 0)
    for a, out in ((0, dk_out), (1, dv_out)):
        accum[a].wait_recv()
        out[...] = acc[1, a] * (1.0 if a else factor) + dkvr[a].astype(f32)

    def drain(r, carry):
        dq_here(r).wait_recv()
        dq_passed(r).wait_recv()
        dq_plane(r).wait_send()
        dq_pass(r).wait_send()
        stat_plane(r).wait_send()
        qg_plane(r).wait_send()
        return carry

    lax.fori_loop(1, 16, drain, 0)
    for c in range(4):
        stat_cross(c).wait_send()
        qg_cross(c).wait_send()
        dq_cross(c).wait_send()
    for i in range(1, 8):
        kv_first(i).wait_send()
    kv_next.wait_send()
    for slot in (0, 1):
        for i in (1, 2, 3):
            kv_cols(slot, i).wait_send()
    for copy in accum:
        copy.wait_send()


def per_device(queries, keys, values, grad_out, stats, placement):
    f32, bf16 = jnp.float32, jnp.bfloat16
    vmem = pl.BlockSpec(memory_space=pltpu.VMEM)
    sem = pltpu.SemaphoreType.DMA
    dq, dk, dv = pl.pallas_call(
        kernel,
        name="exchange_grads",
        out_shape=(
            jax.ShapeDtypeStruct((32, 32, 128), bf16),
            jax.ShapeDtypeStruct((1024, 128), f32),
            jax.ShapeDtypeStruct((1024, 128), f32),
        ),
        in_specs=[pl.BlockSpec(memory_space=pltpu.SMEM)] + [vmem] * 5,
        out_specs=(vmem, vmem, vmem),
        scratch_shapes=[
            pltpu.VMEM((32, 2, 32, 128), bf16),
            pltpu.VMEM((2, 16, 2, 32, 128), bf16),
            pltpu.VMEM((16, 2, 32, 128), bf16),
            pltpu.VMEM((2, 4, 32, 128), bf16),
            pltpu.VMEM((32, 1, 128), f32),
            pltpu.VMEM((2, 16, 1, 128), f32),
            pltpu.VMEM((16, 1, 128), f32),
            pltpu.VMEM((2, 2, 4, 4, 2, 32, 128), bf16),
            pltpu.VMEM((2, 2, 1024, 128), f32),
            pltpu.VMEM((32, 32, 128), bf16),
            pltpu.VMEM((16, 32, 128), bf16),
            pltpu.VMEM((2, 1024, 128), bf16),
            pltpu.VMEM((2, 1024, 128), bf16),
            sem((16,)), sem((16,)), sem((16,)), sem((16,)), sem((4,)), sem((4,)), sem((4,)), sem((4,)),
            sem((8,)), sem((8,)), sem((8,)), sem((8,)), sem((1,)), sem((1,)),
            sem((16,)), sem((16,)), sem((4,)), sem((4,)), sem((16,)), sem((16,)),
            sem((2,)), sem((2,)), sem((3,)),
        ],
        compiler_params=pltpu.CompilerParams(collective_id=0, has_side_effects=True),
    )(placement, queries, grad_out, keys, values, stats.transpose(1, 2, 0))
    return dq.transpose(1, 0, 2), dk[:, None, :], dv[:, None, :]


def solution(mesh):
    tokens = P(("blk", "uly"), None, None)
    return jax.shard_map(
        per_device,
        mesh=mesh,
        in_specs=(tokens,) * 5 + (P(),),
        out_specs=(tokens, P("blk", "uly", None), P("blk", "uly", None)),
        check_vma=False,
    )
```
